32 devices in a mesh: group: 2 (over y), row: 4 (over x, core), col: 4 (over z).
Axes of the slice: x: 2, y: 2, z: 4, core: 2. Of those that a mesh axis runs over, the one named last changes fastest.
Arguments:
- tokens: bfloat16 [4096, 4096], P(('group', 'col'), 'row'), parts along dimension 0, may hold values from -6 to 6
- norm_gain: bfloat16 [4096], replicated, may hold values from 0.099609375 to 1.8984375
- gate_weight: bfloat16 [4096, 14336], P('col', 'row'), may hold values from -0.125 to 0.125
- up_weight: bfloat16 [4096, 14336], P('col', 'row'), may hold values from -0.125 to 0.125
- down_weight: bfloat16 [14336, 4096], P('col', 'row'), may hold values from -0.0625 to 0.0625
- block_mask: int32 [3, 64, 64], replicated, may hold values from 0 to 1, as said below
Outputs:
- mixed: bfloat16 [4096, 4096], P(('group', 'col'), 'row'), parts along dimension 0
The draws below stay inside these ranges and needn't reach their ends.
There are 2 independent parts, one for each index of `group`. The reference program is written for one: setup_inputs(seed, part) draws one part's arguments, and reference() takes and returns one part's arrays. A program takes and returns all parts, laid end to end along the dimension named above; an argument that names none is the same for every part. Nothing has to cross between parts.
Inputs may be any that keep to these rules, and one draw needn't show every extreme that they name: `block_mask`: in every mask and every block column, each aligned group of 16 block rows (those of one index of col) holds 1 to 12 ones, and in every block column some group holds exactly 12.
All inputs are finite; a program needn't handle non-finite values.
Results may differ from the reference program's by a relative error of at most 0.0064.
Values may be sent and summed in bfloat16 or wider, within the bound.
No kernel may reach another device: no remote copies, remote signals or barrier semaphores. Data moves between devices by JAX's collectives and lax.ppermute only.
A program may use at most 256 MiB of HBM per device.

```python
import jax
import jax.numpy as jnp
from jax import lax

D = 4096
FF = 14336
MASK_BLOCKS = 64
TOKENS = 2048
BLK_ROWS = 16
CAP = 12
N_COL = 4


def draw_block_mask(key, part):
    key_count, key_forced, key_score = jax.random.split(key, 3)
    counts = jax.random.randint(key_count, (3, N_COL, MASK_BLOCKS), 1, CAP + 1)
    forced = jax.random.randint(key_forced, (3, MASK_BLOCKS), 0, N_COL)
    groups = jnp.arange(N_COL, dtype=jnp.int32)[None, :, None]
    counts = jnp.where(groups == forced[:, None, :], CAP, counts)
    scores = jax.random.randint(key_score, (3, N_COL, BLK_ROWS, MASK_BLOCKS), 0, 1 << 20)
    scores = scores * BLK_ROWS + jnp.arange(BLK_ROWS, dtype=jnp.int32)[None, None, :, None]
    ranks = jnp.argsort(jnp.argsort(scores, axis=2), axis=2)
    ones = (ranks < counts[:, :, None, :]).astype(jnp.int32)
    return ones.reshape(3, MASK_BLOCKS, MASK_BLOCKS)


def level_of(own_key, dims, cuts, low, largest):
    loudness = 1.0
    for axis_at, parts in cuts:
        steps = jax.random.uniform(jax.random.fold_in(jax.random.fold_in(own_key, 6), axis_at), (parts,), jnp.float32, low / len(cuts), largest / len(cuts))
        loudness = loudness * jnp.repeat(jnp.exp(steps), dims[axis_at] // parts).reshape((-1,) + (1,) * (len(dims) - 1 - axis_at))
    return loudness


def scatter_about(rng, dims, scale, limit, pieces=(), kind=jnp.bfloat16):
    result = jax.random.normal(rng, dims, jnp.float32) * scale
    if len(pieces) > 0:
        result = level_of(rng, dims, pieces, -0.22, 0.18) * result
    return jnp.clip(result, min=-limit, max=limit).astype(kind)


def setup_inputs(seed: int = 0, part: int = 0) -> dict:
    key_of = jax.random.split(jax.random.key(seed), 7)
    part_keys = jax.random.split(jax.random.fold_in(key_of[6], part), 7)
    return {
        "tokens": scatter_about(part_keys[0], (TOKENS, D), 1.0, 6.0, ((0, 4), (1, 4))),
        "norm_gain": jnp.clip(1.0 + 0.18 * jax.random.normal(key_of[1], (D,), jnp.float32), 0.099609375, 1.8984375).astype(jnp.bfloat16),
        "gate_weight": scatter_about(key_of[2], (D, FF), (D // 2) ** -0.5, 0.125, ((0, 4), (1, 4))),
        "up_weight": scatter_about(key_of[3], (D, FF), (D // 2) ** -0.5, 0.125, ((0, 4), (1, 4))),
        "down_weight": scatter_about(key_of[4], (FF, D), (FF // 2) ** -0.5, 0.0625, ((0, 4), (1, 4))),
        "block_mask": draw_block_mask(jax.random.fold_in(key_of[6], 71), part),
    }


def expand_mask(mask, weight):
    tall = weight.shape[0] // MASK_BLOCKS
    broad = weight.shape[1] // MASK_BLOCKS
    full_mask = jnp.repeat(jnp.repeat(mask, tall, axis=0), broad, axis=1)
    return weight * full_mask.astype(weight.dtype)

def reference(tokens, norm_gain, gate_weight, up_weight, down_weight, block_mask):
    values = tokens.astype(jnp.float32)
    square_mean = lax.optimization_barrier(jnp.mean(values * values, axis=-1, keepdims=True))
    normed = (values * lax.rsqrt(square_mean + 1e-05) * norm_gain.astype(jnp.float32)).astype(jnp.bfloat16)
    gate = jnp.dot(normed, expand_mask(block_mask[0], gate_weight), preferred_element_type=jnp.float32)
    up = jnp.dot(normed, expand_mask(block_mask[1], up_weight), preferred_element_type=jnp.float32)
    hidden = (jax.nn.silu(gate) * up).astype(jnp.bfloat16)
    mixed = jnp.dot(hidden, expand_mask(block_mask[2], down_weight), preferred_element_type=jnp.float32)
    return mixed.astype(jnp.bfloat16)
```

```python
import jax
import jax.numpy as jnp
from jax import lax
from jax.experimental import pallas as pl
from jax.experimental.pallas import tpu as pltpu
from jax.sharding import PartitionSpec as P

F32 = jnp.float32
BF16 = jnp.bfloat16


def masked_tile(weight, mask, col_at, row_at, n_col, n_row):
    per_col = mask.shape[0] // n_col
    per_row = mask.shape[1] // n_row
    tile = lax.dynamic_slice(mask, (col_at * per_col, row_at * per_row), (per_col, per_row))
    tall = weight.shape[0] // per_col
    broad = weight.shape[1] // per_row
    shaped = (
        weight.reshape(per_col, tall, per_row, broad) * tile.astype(weight.dtype)[:, None, :, None]
    )
    return shaped.reshape(weight.shape)


def plain_body(tokens, norm_gain, gate_weight, up_weight, down_weight, block_mask):
    n_row = lax.axis_size("row")
    n_col = lax.axis_size("col")
    row_at = lax.axis_index("row")
    col_at = lax.axis_index("col")
    whole = lax.all_gather(tokens, "row", axis=1, tiled=True)
    values = whole.astype(F32)
    square_mean = jnp.mean(values * values, axis=-1, keepdims=True)
    normed = (values * lax.rsqrt(square_mean + 1e-05) * norm_gain.astype(F32)).astype(BF16)
    gate_tile = masked_tile(gate_weight, block_mask[0], col_at, row_at, n_col, n_row)
    up_tile = masked_tile(up_weight, block_mask[1], col_at, row_at, n_col, n_row)
    gate = jnp.dot(
        normed, lax.all_gather(gate_tile, "col", axis=0, tiled=True), preferred_element_type=F32
    )
    up = jnp.dot(
        normed, lax.all_gather(up_tile, "col", axis=0, tiled=True), preferred_element_type=F32
    )
    hidden = (jax.nn.silu(gate) * up).astype(BF16)
    down_tile = masked_tile(down_weight, block_mask[2], col_at, row_at, n_col, n_row)
    down_full = lax.all_gather(down_tile, "col", axis=0, tiled=True)
    mixed = jnp.dot(
        lax.all_gather(hidden, "row", axis=1, tiled=True), down_full, preferred_element_type=F32
    )
    return mixed.astype(BF16)


def cap_of(per_col):
    return per_col * 3 // 4


def lane_parts(tile, broad):
    first = tile * 128 // broad
    last = (tile * 128 + 127) // broad
    return first, last, last * broad - tile * 128


def pack(gate_weight, up_weight, table, where_at, shift, per_col, per_row, n_col, n_blocks):
    rows, cols = gate_weight.shape
    width = cols // n_col
    tall = rows // per_col
    broad = cols // per_row
    cap = cap_of(per_col)
    per_dest = per_row // n_col

    def kernel(table_ref, at_ref, gate_ref, up_ref, out_ref):
        group, row, col = at_ref[0], at_ref[1], at_ref[2]
        dest = lax.rem(col + shift, n_col)
        left = row * per_row + dest * per_dest

        def copy_from(src):
            @pl.loop(0, cap)
            def _(slot):
                base = ((group * n_col + col) * cap + slot) * n_blocks + left
                to = pl.ds(pl.multiple_of(slot * tall, tall), tall)
                for tile in range(width // 128):
                    first, last, cut = lane_parts(tile, broad)
                    lanes = slice(tile * 128, tile * 128 + 128)
                    at = table_ref[base + first]
                    val = src[pl.ds(pl.multiple_of(at * tall, tall), tall), lanes]
                    if last != first:
                        lane = lax.broadcasted_iota(jnp.int32, (1, 128), 1)
                        early = (lane < cut).astype(F32)
                        at = table_ref[base + last]
                        val2 = src[pl.ds(pl.multiple_of(at * tall, tall), tall), lanes]
                        val = val * early.astype(BF16) + val2 * (1.0 - early).astype(BF16)
                    out_ref[to, lanes] = val

        @pl.when(group == 0)
        def _():
            copy_from(gate_ref)

        @pl.when(group != 0)
        def _():
            copy_from(up_ref)

    spec = pl.BlockSpec((rows, width), lambda i, table, at: (0, lax.rem(at[2] + shift, n_col)))
    return pl.pallas_call(
        kernel,
        grid_spec=pltpu.PrefetchScalarGridSpec(
            num_scalar_prefetch=2,
            grid=(1,),
            in_specs=[spec, spec],
            out_specs=pl.BlockSpec((cap * tall, width), lambda i, table, at: (0, 0)),
        ),
        out_shape=jax.ShapeDtypeStruct((cap * tall, width), BF16),
        cost_estimate=pl.CostEstimate(flops=0, bytes_accessed=6 * rows * width, transcendentals=0),
        name=f"pack{shift}",
    )(table, where_at, gate_weight, up_weight)


def expand(mine, other, slots, where_at, shift, dense, sizes):
    rows, width, per_col, per_row, n_col, n_blocks = sizes
    tall = rows // per_col
    per_dest = per_row // n_col
    broad = width // per_dest
    own = shift == 0

    def kernel(slots_ref, at_ref, mine_ref, other_ref, *rest):
        out_ref = rest[-1]
        group, row, col = at_ref[0], at_ref[1], at_ref[2]
        source = lax.rem(col - shift + n_col, n_col)
        left = row * per_row + col * per_dest

        @pl.loop(0, per_col)
        def _(block):
            to = pl.ds(pl.multiple_of(block * tall, tall), tall)
            for which, src in ((0, mine_ref), (1, other_ref)):
                matrix = group if which == 0 else 1 - group
                base = ((matrix * n_col + source) * per_col + block) * n_blocks + left
                for tile in range(width // 128):
                    first, last, cut = lane_parts(tile, broad)
                    lanes = slice(tile * 128, tile * 128 + 128)
                    total = None
                    for part in range(first, last + 1):
                        slot = slots_ref[base + part]
                        keep = jnp.where(slot >= 0, 1.0, 0.0).astype(F32)
                        at = block if own else jnp.maximum(slot, 0)
                        val = src[pl.ds(pl.multiple_of(at * tall, tall), tall), lanes]
                        weight = jnp.full((1, 128), keep, F32)
                        if last != first:
                            lane = lax.broadcasted_iota(jnp.int32, (1, 128), 1)
                            side = lane < cut if part == first else lane >= cut
                            weight = jnp.where(side, weight, 0.0)
                        val = val * weight.astype(BF16)
                        total = val if total is None else total + val
                    start = tile * 256 + which * 128
                    out_ref[0, to, start : start + 128] = total

    src_spec = [pl.BlockSpec(mine.shape, lambda i, slots, at: (0, 0))] * 2
    args = [slots, where_at, mine, other]
    aliases = {}
    if dense is not None:
        args.append(dense)
        src_spec = src_spec + [pl.BlockSpec(memory_space=pl.ANY)]
        aliases = {4: 0}
    return pl.pallas_call(
        kernel,
        grid_spec=pltpu.PrefetchScalarGridSpec(
            num_scalar_prefetch=2,
            grid=(1,),
            in_specs=src_spec,
            out_specs=pl.BlockSpec(
                (1, rows, 2 * width),
                lambda i, slots, at: (lax.rem(at[2] - shift + n_col, n_col), 0, 0),
            ),
        ),
        out_shape=jax.ShapeDtypeStruct((n_col, rows, 2 * width), BF16),
        input_output_aliases=aliases,
        cost_estimate=pl.CostEstimate(flops=0, bytes_accessed=8 * rows * width, transcendentals=0),
        name=f"expand{shift}",
    )(*args)


def gate_up(pieces, dense, where_at, name):
    tokens, depth = pieces[0].shape
    n_col, rows, double = dense.shape
    tiles = double // 256

    def kernel(at_ref, x0, x1, x2, x3, w_ref, out_ref):
        group, row = at_ref[0], at_ref[1]
        total = None
        for m, x in enumerate((x0, x1, x2, x3)):
            part = jnp.dot(x[...], w_ref[row ^ m], preferred_element_type=F32)
            total = part if total is None else total + part
        mine, other = total[:, :128], total[:, 128:]
        gate = jnp.where(group == 0, mine, other)
        up = jnp.where(group == 0, other, mine)
        out_ref[...] = (gate / (1.0 + jnp.exp(-gate)) * up).astype(BF16)

    return pl.pallas_call(
        kernel,
        grid_spec=pltpu.PrefetchScalarGridSpec(
            num_scalar_prefetch=1,
            grid=(tiles,),
            in_specs=[pl.BlockSpec((tokens, depth), lambda n, at: (0, 0))] * 4
            + [pl.BlockSpec((n_col, rows, 256), lambda n, at: (0, 0, n))],
            out_specs=pl.BlockSpec((tokens, 128), lambda n, at: (0, n)),
        ),
        out_shape=jax.ShapeDtypeStruct((tokens, tiles * 128), BF16),
        cost_estimate=pl.CostEstimate(
            flops=2 * tokens * n_col * rows * double,
            bytes_accessed=2 * (4 * tokens * depth + dense.size),
            transcendentals=tokens * tiles * 128,
        ),
        name=name,
    )(where_at, *pieces, dense)


def down_part(pieces, weights, where_at, so_far, name):
    tokens, depth = pieces[0].shape
    n_col, _, _, half = weights.shape

    def kernel(at_ref, h0, h1, h2, h3, w_ref, *rest):
        out_ref = rest[-1]
        row, col = at_ref[1], at_ref[2]
        total = None
        for m, h in enumerate((h0, h1, h2, h3)):
            at = lax.rem(col - (row ^ m) + n_col, n_col)
            part = jnp.dot(h[...], w_ref[at, 0], preferred_element_type=F32)
            total = part if total is None else total + part
        if so_far is not None:
            total = total + rest[0][...].astype(F32)
        out_ref[...] = total.astype(BF16)

    extra = [] if so_far is None else [so_far]
    out_spec = pl.BlockSpec((tokens, half), lambda n, at: (0, n))
    return pl.pallas_call(
        kernel,
        grid_spec=pltpu.PrefetchScalarGridSpec(
            num_scalar_prefetch=1,
            grid=(2,),
            in_specs=[pl.BlockSpec((tokens, depth), lambda n, at: (0, 0))] * 4
            + [pl.BlockSpec((n_col, 1, depth, half), lambda n, at: (0, n ^ at[0], 0, 0))]
            + [out_spec] * len(extra),
            out_specs=out_spec,
        ),
        out_shape=jax.ShapeDtypeStruct((tokens, 2 * half), BF16),
        cost_estimate=pl.CostEstimate(
            flops=4 * tokens * n_col * depth * half,
            bytes_accessed=2 * (4 * tokens * depth + weights.size + tokens * half * 2),
            transcendentals=0,
        ),
        name=name,
    )(where_at, *pieces, weights, *extra)


def body(tokens, norm_gain, gate_weight, up_weight, down_weight, block_mask):
    n_row = lax.axis_size("row")
    n_col = lax.axis_size("col")
    group = lax.axis_index("group")
    row = lax.axis_index("row")
    col = lax.axis_index("col")
    n_blocks = block_mask.shape[-1]
    per_col = n_blocks // n_col
    per_row = n_blocks // n_row
    cap = cap_of(per_col)
    rows, cols = gate_weight.shape
    width = cols // n_col

    def along(axis, shift):
        size = lax.axis_size(axis)
        pairs = [(i, (i + shift) % size) for i in range(size)]
        return lambda v: lax.ppermute(v, axis, pairs)

    def by_xor(bit):
        pairs = [(i, i ^ bit) for i in range(n_row)]
        return lambda v: lax.ppermute(v, "row", pairs)

    z = {s: along("col", s) for s in range(1, n_col)}
    y_swap = along("group", 1)
    core_swap = by_xor(1)
    x_swap = by_xor(2)

    three = lax.iota(jnp.int32, 3)
    where_at = jnp.where(three == 0, group, jnp.where(three == 1, row, col)).astype(jnp.int32)
    grouped = block_mask[:2].reshape(2, n_col, per_col, n_blocks)
    ids = jnp.arange(per_col, dtype=jnp.int32)
    before = (ids[None, :] < ids[:, None]).astype(jnp.int32)
    rank = jnp.sum(before[None, None, :, :, None] * grouped[:, :, None, :, :], axis=3)
    slots = jnp.where(grouped > 0, rank, -1).astype(jnp.int32)
    wanted = jnp.arange(cap, dtype=jnp.int32)
    table = jnp.sum(
        jnp.where(
            slots[:, :, None, :, :] == wanted[None, None, :, None, None],
            ids[None, None, None, :, None],
            0,
        ),
        axis=3,
    ).astype(jnp.int32)
    slots = slots.reshape(-1)
    table = table.reshape(-1)

    values = tokens.astype(F32)
    squares = jnp.sum(values * values, axis=-1)
    squares = squares + core_swap(squares)
    squares = squares + x_swap(squares)
    depth = tokens.shape[1]
    gain = lax.dynamic_slice(norm_gain, (row * depth,), (depth,)).astype(F32)
    mean = (squares / norm_gain.shape[0])[:, None]
    normed = (values * lax.rsqrt(mean + 1e-05) * gain).astype(BF16)
    shards = [normed]
    for _ in range(n_col - 1):
        shards.append(z[1](shards[-1]))

    def over_row(v):
        across = x_swap(v)
        return v, core_swap(v), across, core_swap(across)

    chunks = [over_row(v) for v in shards]

    sizes = (rows, width, per_col, per_row, n_col, n_blocks)
    order = [s for s in range(1, n_col) if 2 * s != n_col] + [n_col // 2]
    dense = None
    mine = {}
    for s in order:
        packed = pack(
            gate_weight, up_weight, table, where_at, s, per_col, per_row, n_col, n_blocks
        )
        mine[s] = z[s](packed)
    first = jnp.where(group == 0, 1, 0) > 0
    own_gate = lax.dynamic_slice(gate_weight, (0, col * width), (rows, width))
    own_up = lax.dynamic_slice(up_weight, (0, col * width), (rows, width))
    own_mine = jnp.where(first, own_gate, own_up)
    own_other = jnp.where(first, own_up, own_gate)
    dense = expand_own(own_mine, own_other, slots, where_at, sizes)
    for s in order:
        dense = expand(mine[s], y_swap(mine[s]), slots, where_at, s, dense, sizes)

    down_rows = down_weight.shape[0] // n_col
    half = down_weight.shape[1] // 2
    tile = lax.dynamic_slice(block_mask[2], (col * per_col, row * per_row), (per_col, per_row))
    wide = jnp.repeat(tile.astype(BF16), down_weight.shape[1] // per_row, axis=1)
    sub = per_col // n_col

    def down_piece(dest, side):
        at = (dest * down_rows, side * half)
        block = lax.dynamic_slice(down_weight, at, (down_rows, half))
        ones = lax.dynamic_slice(wide, (dest * sub, side * half), (sub, half))
        return (block.reshape(sub, -1, half) * ones[:, None, :]).reshape(down_rows, half)

    parts = [[down_piece(col, group), down_piece(col, 1 - group)]] + [None] * (n_col - 1)
    for s in order:
        got = z[s](down_piece(lax.rem(col + s, n_col), group))
        parts[s] = [got, y_swap(got)]
    weights = jnp.stack([v for pair in parts for v in pair]).reshape(n_col, 2, down_rows, half)

    so_far = None
    for s in list(range(1, n_col)) + [0]:
        hidden = gate_up(chunks[s], dense, where_at, f"gate_up{s}")
        out = down_part(over_row(hidden), weights, where_at, so_far, f"down{s}")
        so_far = z[1](out) if s else out
    return so_far


def expand_own(own_mine, own_other, slots, where_at, sizes):
    return expand(own_mine, own_other, slots, where_at, 0, None, sizes)


def solution(mesh):
    in_specs = (
        P(("group", "col"), "row"),
        P(),
        P("col", "row"),
        P("col", "row"),
        P("col", "row"),
        P(),
    )
    out_specs = P(("group", "col"), "row")
    sizes = dict(mesh.shape)
    fits = sizes["row"] == 4 and sizes["col"] == 4 and sizes["group"] == 2

    def step(tokens, norm_gain, gate_weight, up_weight, down_weight, block_mask):
        lanes = gate_weight.shape[1] // (sizes["row"] * sizes["col"])
        chosen = body if fits and lanes % 128 == 0 else plain_body
        return jax.shard_map(
            chosen, mesh=mesh, in_specs=in_specs, out_specs=out_specs, check_vma=False
        )(tokens, norm_gain, gate_weight, up_weight, down_weight, block_mask)

    return step
```

```python
import jax
import jax.numpy as jnp
from jax import lax
from jax.experimental import pallas as pl
from jax.experimental.pallas import tpu as pltpu
from jax.sharding import PartitionSpec as P


F32 = jnp.float32
BF16 = jnp.bfloat16


def masked_tile(weight, mask, col_at, row_at, n_col, n_row):
    per_col = mask.shape[0] // n_col
    per_row = mask.shape[1] // n_row
    tile = lax.dynamic_slice(mask, (col_at * per_col, row_at * per_row), (per_col, per_row))
    tall = weight.shape[0] // per_col
    broad = weight.shape[1] // per_row
    shaped = (
        weight.reshape(per_col, tall, per_row, broad) * tile.astype(weight.dtype)[:, None, :, None]
    )
    return shaped.reshape(weight.shape)


def plain_body(tokens, norm_gain, gate_weight, up_weight, down_weight, block_mask):
    n_row = lax.axis_size("row")
    n_col = lax.axis_size("col")
    row_at = lax.axis_index("row")
    col_at = lax.axis_index("col")
    whole = lax.all_gather(tokens, "row", axis=1, tiled=True)
    values = whole.astype(F32)
    square_mean = jnp.mean(values * values, axis=-1, keepdims=True)
    normed = (values * lax.rsqrt(square_mean + 1e-05) * norm_gain.astype(F32)).astype(BF16)
    gate_tile = masked_tile(gate_weight, block_mask[0], col_at, row_at, n_col, n_row)
    up_tile = masked_tile(up_weight, block_mask[1], col_at, row_at, n_col, n_row)
    gate = jnp.dot(
        normed, lax.all_gather(gate_tile, "col", axis=0, tiled=True), preferred_element_type=F32
    )
    up = jnp.dot(
        normed, lax.all_gather(up_tile, "col", axis=0, tiled=True), preferred_element_type=F32
    )
    hidden = (jax.nn.silu(gate) * up).astype(BF16)
    down_tile = masked_tile(down_weight, block_mask[2], col_at, row_at, n_col, n_row)
    down_full = lax.all_gather(down_tile, "col", axis=0, tiled=True)
    mixed = jnp.dot(
        lax.all_gather(hidden, "row", axis=1, tiled=True), down_full, preferred_element_type=F32
    )
    return mixed.astype(BF16)


def cap_of(per_col):
    return per_col * 3 // 4


def lane_parts(tile, broad):
    first = tile * 128 // broad
    last = (tile * 128 + 127) // broad
    return first, last, last * broad - tile * 128


def pack(gate_weight, up_weight, table, where_at, m, per_col, per_row, n_col, n_blocks):
    rows, cols = gate_weight.shape
    width = cols // n_col
    tall = rows // per_col
    broad = cols // per_row
    cap = cap_of(per_col)
    per_dest = per_row // n_col
    half = cap // 2

    def kernel(table_ref, at_ref, gate_ref, up_ref, low_ref, high_ref):
        group, row, col = at_ref[0], at_ref[1], at_ref[2]
        left = row * per_row + (row ^ col ^ m) * per_dest

        def copy_from(src):
            for side, out_ref in enumerate((low_ref, high_ref)):

                @pl.loop(0, half)
                def _(step):
                    slot = step + side * half
                    base = ((group * n_col + col) * cap + slot) * n_blocks + left
                    to = pl.ds(pl.multiple_of(step * tall, tall), tall)
                    for tile in range(width // 128):
                        first, last, cut = lane_parts(tile, broad)
                        lanes = slice(tile * 128, tile * 128 + 128)
                        at = table_ref[base + first]
                        val = src[pl.ds(pl.multiple_of(at * tall, tall), tall), lanes]
                        if last != first:
                            lane = lax.broadcasted_iota(jnp.int32, (1, 128), 1)
                            early = (lane < cut).astype(F32)
                            at = table_ref[base + last]
                            val2 = src[pl.ds(pl.multiple_of(at * tall, tall), tall), lanes]
                            val = val * early.astype(BF16) + val2 * (1.0 - early).astype(BF16)
                        out_ref[to, lanes] = val

        @pl.when(group == 0)
        def _():
            copy_from(gate_ref)

        @pl.when(group != 0)
        def _():
            copy_from(up_ref)

    spec = pl.BlockSpec((rows, width), lambda i, table, at: (0, at[1] ^ at[2] ^ m))
    shape = (half * tall, width)
    return pl.pallas_call(
        kernel,
        grid_spec=pltpu.PrefetchScalarGridSpec(
            num_scalar_prefetch=2,
            grid=(1,),
            in_specs=[spec, spec],
            out_specs=[pl.BlockSpec(shape, lambda i, table, at: (0, 0))] * 2,
        ),
        out_shape=[jax.ShapeDtypeStruct(shape, BF16)] * 2,
        cost_estimate=pl.CostEstimate(flops=0, bytes_accessed=6 * rows * width, transcendentals=0),
    )(table, where_at, gate_weight, up_weight)


def expand(mine, other, slots, where_at, m, dense, sizes):
    rows, width, per_col, per_row, n_col, n_blocks = sizes
    tall = rows // per_col
    per_dest = per_row // n_col
    broad = width // per_dest
    part_rows = mine[0].shape[0]

    def kernel(slots_ref, at_ref, *refs):
        parts, out_ref, held, sems = refs[:4], refs[-3], refs[-2], refs[-1]
        copies = [
            pltpu.make_async_copy(
                part, held.at[i // 2, pl.ds((i % 2) * part_rows, part_rows)], sems.at[i]
            )
            for i, part in enumerate(parts)
        ]
        for copy in copies:
            copy.start()
        for copy in copies:
            copy.wait()
        group, row, col = at_ref[0], at_ref[1], at_ref[2]
        source = row ^ col ^ m
        left = col * per_row + row * per_dest

        @pl.loop(0, per_col)
        def _(block):
            to = pl.ds(pl.multiple_of(block * tall, tall), tall)
            for which in range(2):
                matrix = group if which == 0 else 1 - group
                base = ((matrix * n_col + source) * per_col + block) * n_blocks + left
                for tile in range(width // 128):
                    first, last, cut = lane_parts(tile, broad)
                    lanes = slice(tile * 128, tile * 128 + 128)
                    total = None
                    for part in range(first, last + 1):
                        slot = slots_ref[base + part]
                        keep = jnp.where(slot >= 0, 1.0, 0.0).astype(F32)
                        at = jnp.maximum(slot, 0)
                        val = held[which, pl.ds(pl.multiple_of(at * tall, tall), tall), lanes]
                        weight = jnp.full((1, 128), keep, F32)
                        if last != first:
                            lane = lax.broadcasted_iota(jnp.int32, (1, 128), 1)
                            side = lane < cut if part == first else lane >= cut
                            weight = jnp.where(side, weight, 0.0)
                        val = val * weight.astype(BF16)
                        total = val if total is None else total + val
                    start = tile * 256 + which * 128
                    out_ref[0, to, start : start + 128] = total

    args = [slots, where_at, *mine, *other]
    any_spec = pl.BlockSpec(memory_space=pl.ANY)
    specs = [any_spec] * 4
    aliases = {}
    if dense is not None:
        args.append(dense)
        specs.append(any_spec)
        aliases = {6: 0}
    return pl.pallas_call(
        kernel,
        grid_spec=pltpu.PrefetchScalarGridSpec(
            num_scalar_prefetch=2,
            grid=(1,),
            in_specs=specs,
            out_specs=pl.BlockSpec(
                (1, rows, 2 * width), lambda i, slots, at: (at[1] ^ at[2] ^ m, 0, 0)
            ),
            scratch_shapes=[
                pltpu.VMEM((2, 2 * part_rows, width), BF16),
                pltpu.SemaphoreType.DMA((4,)),
            ],
        ),
        out_shape=jax.ShapeDtypeStruct((n_col, rows, 2 * width), BF16),
        input_output_aliases=aliases,
        cost_estimate=pl.CostEstimate(flops=0, bytes_accessed=8 * rows * width, transcendentals=0),
    )(*args)


def norm_of(pieces, gain, where_at):
    tokens, depth = pieces[0].shape
    tall = tokens // 4

    def kernel(at_ref, p0, p1, p2, p3, gain_ref, out_ref):
        row = at_ref[1]
        parts = [p[...].astype(F32) for p in (p0, p1, p2, p3)]
        squares = sum(jnp.sum(v * v, axis=-1, keepdims=True) for v in parts)
        scale = lax.rsqrt(squares / (4 * depth) + 1e-05)
        for m, v in enumerate(parts):
            at = row ^ m
            normed = v * scale * gain_ref[at].astype(F32)
            out_ref[:, pl.ds(pl.multiple_of(at * depth, 128), depth)] = normed.astype(BF16)

    return pl.pallas_call(
        kernel,
        grid_spec=pltpu.PrefetchScalarGridSpec(
            num_scalar_prefetch=1,
            grid=(4,),
            in_specs=[pl.BlockSpec((tall, depth), lambda n, at: (n, 0))] * 4
            + [pl.BlockSpec((4, 1, depth), lambda n, at: (0, 0, 0))],
            out_specs=pl.BlockSpec((tall, 4 * depth), lambda n, at: (n, 0)),
        ),
        out_shape=jax.ShapeDtypeStruct((tokens, 4 * depth), BF16),
        cost_estimate=pl.CostEstimate(
            flops=4 * tokens * depth * 4, bytes_accessed=16 * tokens * depth, transcendentals=tokens
        ),
    )(where_at, *pieces, gain.reshape(4, 1, depth))


def mask_down(weight, wide):
    blocks, _, cols = wide.shape
    tall = weight.shape[0] // blocks

    def kernel(w_ref, mask_ref, out_ref):
        out_ref[...] = w_ref[...] * mask_ref[0]

    return pl.pallas_call(
        kernel,
        grid=(blocks,),
        in_specs=[
            pl.BlockSpec((tall, cols), lambda n: (n, 0)),
            pl.BlockSpec((1, 1, cols), lambda n: (n, 0, 0)),
        ],
        out_specs=pl.BlockSpec((tall, cols), lambda n: (n, 0)),
        out_shape=jax.ShapeDtypeStruct(weight.shape, BF16),
        cost_estimate=pl.CostEstimate(
            flops=weight.size, bytes_accessed=4 * weight.size, transcendentals=0
        ),
    )(weight, wide)


def gate_up(x, dense, where_at):
    tokens, depth = x.shape
    double = dense.shape[1]
    tiles = double // 256

    def kernel(at_ref, x_ref, w_ref, out_ref):
        total = jnp.dot(x_ref[...], w_ref[...], preferred_element_type=F32)
        mine, other = total[:, :128], total[:, 128:]
        gate = jnp.where(at_ref[0] == 0, mine, other)
        up = jnp.where(at_ref[0] == 0, other, mine)
        out_ref[...] = (gate / (1.0 + jnp.exp(-gate)) * up).astype(BF16)

    return pl.pallas_call(
        kernel,
        grid_spec=pltpu.PrefetchScalarGridSpec(
            num_scalar_prefetch=1,
            grid=(tiles,),
            in_specs=[
                pl.BlockSpec((tokens, depth), lambda n, at: (0, 0)),
                pl.BlockSpec((depth, 256), lambda n, at: (0, n)),
            ],
            out_specs=pl.BlockSpec((tokens, 128), lambda n, at: (0, n)),
        ),
        out_shape=jax.ShapeDtypeStruct((tokens, tiles * 128), BF16),
        cost_estimate=pl.CostEstimate(
            flops=2 * tokens * depth * double,
            bytes_accessed=2 * (tokens * depth + dense.size),
            transcendentals=tokens * tiles * 128,
        ),
    )(where_at, x, dense)


def down_part(pieces, weights, where_at, kind):
    tokens, depth = pieces[0].shape
    n_row, _, cols = weights.shape
    lanes = 256

    def kernel(at_ref, h0, h1, h2, h3, w_ref, out_ref):
        row = at_ref[1]
        total = None
        for m, h in enumerate((h0, h1, h2, h3)):
            part = jnp.dot(h[...], w_ref[row ^ m], preferred_element_type=F32)
            total = part if total is None else total + part
        out_ref[...] = total.astype(kind)

    out_spec = pl.BlockSpec((tokens, lanes), lambda n, at: (0, n))
    return pl.pallas_call(
        kernel,
        grid_spec=pltpu.PrefetchScalarGridSpec(
            num_scalar_prefetch=1,
            grid=(cols // lanes,),
            in_specs=[pl.BlockSpec((tokens, depth), lambda n, at: (0, 0))] * 4
            + [pl.BlockSpec((n_row, depth, lanes), lambda n, at: (0, 0, n))],
            out_specs=out_spec,
        ),
        out_shape=jax.ShapeDtypeStruct((tokens, cols), kind),
        cost_estimate=pl.CostEstimate(
            flops=2 * tokens * n_row * depth * cols,
            bytes_accessed=2 * (4 * tokens * depth + weights.size + tokens * cols * 2),
            transcendentals=0,
        ),
    )(where_at, *pieces, weights)


def body(*args):
    return layer(*args)


def layer(tokens, norm_gain, gate_weight, up_weight, down_weight, block_mask):
    n_row = lax.axis_size("row")
    n_col = lax.axis_size("col")
    group = lax.axis_index("group")
    row = lax.axis_index("row")
    col = lax.axis_index("col")
    n_blocks = block_mask.shape[-1]
    per_col = n_blocks // n_col
    per_row = n_blocks // n_row
    cap = cap_of(per_col)
    rows, cols = gate_weight.shape
    width = cols // n_col

    def beside(by):
        return [(i, i ^ by) for i in range(n_col)]

    swap = [(0, 1), (1, 0)]
    core = [(i, i ^ 1) for i in range(n_row)]
    across = [(i, i ^ 2) for i in range(n_row)]
    grid = [(r, c) for r in range(n_row) for c in range(n_col)]

    def in_plane(m):
        return [(r * n_col + c, (r ^ c ^ m) * n_col + c) for r, c in grid if c != m]

    def to_plane(m):
        return [(r * n_col + c, r * n_col + (r ^ c ^ m)) for r, c in grid if r != m]

    three = lax.iota(jnp.int32, 3)
    where_at = jnp.where(three == 0, group, jnp.where(three == 1, row, col)).astype(jnp.int32)
    grouped = block_mask[:2].reshape(2, n_col, per_col, n_blocks)
    ids = jnp.arange(per_col, dtype=jnp.int32)
    before = (ids[None, :] < ids[:, None]).astype(jnp.int32)
    rank = jnp.sum(before[None, None, :, :, None] * grouped[:, :, None, :, :], axis=3)
    slots = jnp.where(grouped > 0, rank, -1).astype(jnp.int32)
    wanted = jnp.arange(cap, dtype=jnp.int32)
    table = jnp.sum(
        jnp.where(
            slots[:, :, None, :, :] == wanted[None, None, :, None, None],
            ids[None, None, None, :, None],
            0,
        ),
        axis=3,
    ).astype(jnp.int32)
    slots = slots.reshape(-1)
    table = table.reshape(-1)

    far = lax.ppermute(tokens, "col", beside(2))
    near = lax.ppermute(tokens, "col", beside(1))
    shards = [tokens, near, far, lax.ppermute(far, "col", beside(1))]

    def over_row(v):
        far = lax.ppermute(v, "row", across)
        return v, lax.ppermute(v, "row", core), far, lax.ppermute(far, "row", core)

    normed = [norm_of(over_row(v), norm_gain, where_at) for v in shards]

    sizes = (rows, width, per_col, per_row, n_col, n_blocks)
    order = [0, 2, 1, 3]
    got = {}
    for m in order:
        halves = pack(gate_weight, up_weight, table, where_at, m, per_col, per_row, n_col, n_blocks)
        got[m] = []
        for v in halves:
            v = jnp.where(col == m, v, lax.ppermute(v, ("row", "col"), in_plane(m)))
            came = lax.ppermute(v, ("row", "col"), to_plane(m))
            v = jnp.where(row == m, v, came)
            got[m].append((v, lax.ppermute(v, "group", swap)))
    dense = None
    for m in order:
        (a, b), (c, d) = got[m]
        dense = expand((a, c), (b, d), slots, where_at, m, dense, sizes)
    dense = dense.reshape(-1, dense.shape[-1])

    tile = lax.dynamic_slice(block_mask[2], (col * per_col, row * per_row), (per_col, per_row))
    wide = jnp.repeat(tile.astype(BF16), down_weight.shape[1] // per_row, axis=1)
    weights = mask_down(down_weight, wide[:, None, :])
    weights = weights.reshape(n_row, -1, down_weight.shape[1])

    def part_of(j, kind):
        hidden = gate_up(normed[j], dense, where_at)
        return down_part(over_row(hidden), weights, where_at, kind)

    passing = lax.ppermute(part_of(3, BF16), "col", beside(1))
    passing = (part_of(2, F32) + passing.astype(F32)).astype(BF16)
    passing = lax.ppermute(passing, "col", beside(2))
    close = lax.ppermute(part_of(1, BF16), "col", beside(1))
    return (part_of(0, F32) + passing.astype(F32) + close.astype(F32)).astype(BF16)


def solution(mesh):
    in_specs = (
        P(("group", "col"), "row"),
        P(),
        P("col", "row"),
        P("col", "row"),
        P("col", "row"),
        P(),
    )
    out_specs = P(("group", "col"), "row")
    sizes = dict(mesh.shape)
    fits = sizes["row"] == 4 and sizes["col"] == 4 and sizes["group"] == 2

    def step(tokens, norm_gain, gate_weight, up_weight, down_weight, block_mask):
        lanes = gate_weight.shape[1] // (sizes["row"] * sizes["col"])
        chosen = body if fits and lanes % 128 == 0 else plain_body
        return jax.shard_map(
            chosen, mesh=mesh, in_specs=in_specs, out_specs=out_specs, check_vma=False
        )(tokens, norm_gain, gate_weight, up_weight, down_weight, block_mask)

    return step
```

```python
import jax
import jax.numpy as jnp
from jax import lax
from jax.experimental import pallas as pl
from jax.experimental.pallas import tpu as pltpu
from jax.sharding import PartitionSpec as P


F32 = jnp.float32
BF16 = jnp.bfloat16


def masked_tile(weight, mask, col_at, row_at, n_col, n_row):
    per_col = mask.shape[0] // n_col
    per_row = mask.shape[1] // n_row
    tile = lax.dynamic_slice(mask, (col_at * per_col, row_at * per_row), (per_col, per_row))
    tall = weight.shape[0] // per_col
    broad = weight.shape[1] // per_row
    shaped = (
        weight.reshape(per_col, tall, per_row, broad) * tile.astype(weight.dtype)[:, None, :, None]
    )
    return shaped.reshape(weight.shape)


def plain_body(tokens, norm_gain, gate_weight, up_weight, down_weight, block_mask):
    n_row = lax.axis_size("row")
    n_col = lax.axis_size("col")
    row_at = lax.axis_index("row")
    col_at = lax.axis_index("col")
    whole = lax.all_gather(tokens, "row", axis=1, tiled=True)
    values = whole.astype(F32)
    square_mean = jnp.mean(values * values, axis=-1, keepdims=True)
    normed = (values * lax.rsqrt(square_mean + 1e-05) * norm_gain.astype(F32)).astype(BF16)
    gate_tile = masked_tile(gate_weight, block_mask[0], col_at, row_at, n_col, n_row)
    up_tile = masked_tile(up_weight, block_mask[1], col_at, row_at, n_col, n_row)
    gate = jnp.dot(
        normed, lax.all_gather(gate_tile, "col", axis=0, tiled=True), preferred_element_type=F32
    )
    up = jnp.dot(
        normed, lax.all_gather(up_tile, "col", axis=0, tiled=True), preferred_element_type=F32
    )
    hidden = (jax.nn.silu(gate) * up).astype(BF16)
    down_tile = masked_tile(down_weight, block_mask[2], col_at, row_at, n_col, n_row)
    down_full = lax.all_gather(down_tile, "col", axis=0, tiled=True)
    mixed = jnp.dot(
        lax.all_gather(hidden, "row", axis=1, tiled=True), down_full, preferred_element_type=F32
    )
    return mixed.astype(BF16)


def cap_of(per_col):
    return per_col * 3 // 4


def lane_parts(tile, broad):
    first = tile * 128 // broad
    last = (tile * 128 + 127) // broad
    return first, last, last * broad - tile * 128


def pack(gate_weight, up_weight, table, where_at, m, per_col, per_row, n_col, n_blocks):
    rows, cols = gate_weight.shape
    width = cols // n_col
    tall = rows // per_col
    broad = cols // per_row
    cap = cap_of(per_col)
    per_dest = per_row // n_col
    half = cap // 2

    def kernel(table_ref, at_ref, gate_ref, up_ref, low_ref, high_ref):
        group, row, col = at_ref[0], at_ref[1], at_ref[2]
        left = row * per_row + (row ^ col ^ m) * per_dest

        def copy_from(src):
            for side, out_ref in enumerate((low_ref, high_ref)):

                @pl.loop(0, half)
                def _(step):
                    slot = step + side * half
                    base = ((group * n_col + col) * cap + slot) * n_blocks + left
                    to = pl.ds(pl.multiple_of(step * tall, tall), tall)
                    for tile in range(width // 128):
                        first, last, cut = lane_parts(tile, broad)
                        lanes = slice(tile * 128, tile * 128 + 128)
                        at = table_ref[base + first]
                        val = src[pl.ds(pl.multiple_of(at * tall, tall), tall), lanes]
                        if last != first:
                            lane = lax.broadcasted_iota(jnp.int32, (1, 128), 1)
                            early = (lane < cut).astype(F32)
                            at = table_ref[base + last]
                            val2 = src[pl.ds(pl.multiple_of(at * tall, tall), tall), lanes]
                            val = val * early.astype(BF16) + val2 * (1.0 - early).astype(BF16)
                        out_ref[to, lanes] = val

        @pl.when(group == 0)
        def _():
            copy_from(gate_ref)

        @pl.when(group != 0)
        def _():
            copy_from(up_ref)

    spec = pl.BlockSpec((rows, width), lambda i, table, at: (0, at[1] ^ at[2] ^ m))
    shape = (half * tall, width)
    return pl.pallas_call(
        kernel,
        grid_spec=pltpu.PrefetchScalarGridSpec(
            num_scalar_prefetch=2,
            grid=(1,),
            in_specs=[spec, spec],
            out_specs=[pl.BlockSpec(shape, lambda i, table, at: (0, 0))] * 2,
        ),
        out_shape=[jax.ShapeDtypeStruct(shape, BF16)] * 2,
        cost_estimate=pl.CostEstimate(flops=0, bytes_accessed=6 * rows * width, transcendentals=0),
    )(table, where_at, gate_weight, up_weight)


def expand(mine, other, slots, where_at, m, dense, sizes):
    rows, width, per_col, per_row, n_col, n_blocks = sizes
    tall = rows // per_col
    per_dest = per_row // n_col
    broad = width // per_dest
    part_rows = mine[0].shape[0]

    def kernel(slots_ref, at_ref, *refs):
        parts, out_ref, held, sems = refs[:4], refs[-3], refs[-2], refs[-1]
        copies = [
            pltpu.make_async_copy(
                part, held.at[i // 2, pl.ds((i % 2) * part_rows, part_rows)], sems.at[i]
            )
            for i, part in enumerate(parts)
        ]
        for copy in copies:
            copy.start()
        for copy in copies:
            copy.wait()
        group, row, col = at_ref[0], at_ref[1], at_ref[2]
        source = row ^ col ^ m
        left = col * per_row + row * per_dest

        @pl.loop(0, per_col)
        def _(block):
            to = pl.ds(pl.multiple_of(block * tall, tall), tall)
            for which in range(2):
                matrix = group if which == 0 else 1 - group
                base = ((matrix * n_col + source) * per_col + block) * n_blocks + left
                for tile in range(width // 128):
                    first, last, cut = lane_parts(tile, broad)
                    lanes = slice(tile * 128, tile * 128 + 128)
                    total = None
                    for part in range(first, last + 1):
                        slot = slots_ref[base + part]
                        keep = jnp.where(slot >= 0, 1.0, 0.0).astype(F32)
                        at = jnp.maximum(slot, 0)
                        val = held[which, pl.ds(pl.multiple_of(at * tall, tall), tall), lanes]
                        weight = jnp.full((1, 128), keep, F32)
                        if last != first:
                            lane = lax.broadcasted_iota(jnp.int32, (1, 128), 1)
                            side = lane < cut if part == first else lane >= cut
                            weight = jnp.where(side, weight, 0.0)
                        val = val * weight.astype(BF16)
                        total = val if total is None else total + val
                    start = tile * 256 + which * 128
                    out_ref[0, to, start : start + 128] = total

    args = [slots, where_at, *mine, *other]
    any_spec = pl.BlockSpec(memory_space=pl.ANY)
    specs = [any_spec] * 4
    aliases = {}
    if dense is not None:
        args.append(dense)
        specs.append(any_spec)
        aliases = {6: 0}
    return pl.pallas_call(
        kernel,
        grid_spec=pltpu.PrefetchScalarGridSpec(
            num_scalar_prefetch=2,
            grid=(1,),
            in_specs=specs,
            out_specs=pl.BlockSpec(
                (1, rows, 2 * width), lambda i, slots, at: (at[1] ^ at[2] ^ m, 0, 0)
            ),
            scratch_shapes=[
                pltpu.VMEM((2, 2 * part_rows, width), BF16),
                pltpu.SemaphoreType.DMA((4,)),
            ],
        ),
        out_shape=jax.ShapeDtypeStruct((n_col, rows, 2 * width), BF16),
        input_output_aliases=aliases,
        cost_estimate=pl.CostEstimate(flops=0, bytes_accessed=8 * rows * width, transcendentals=0),
    )(*args)


def norm_of(pieces, gain, where_at, j, stack):
    tokens, depth = pieces[0].shape
    tall = tokens // 4

    def kernel(at_ref, p0, p1, p2, p3, gain_ref, *rest):
        out_ref = rest[-1]
        row = at_ref[1]
        parts = [p[...].astype(F32) for p in (p0, p1, p2, p3)]
        squares = sum(jnp.sum(v * v, axis=-1, keepdims=True) for v in parts)
        scale = lax.rsqrt(squares / (4 * depth) + 1e-05)
        for m, v in enumerate(parts):
            at = row ^ m
            normed = v * scale * gain_ref[at].astype(F32)
            out_ref[:, pl.ds(pl.multiple_of(at * depth, 128), depth)] = normed.astype(BF16)

    before = [] if stack is None else [stack]
    return pl.pallas_call(
        kernel,
        grid_spec=pltpu.PrefetchScalarGridSpec(
            num_scalar_prefetch=1,
            grid=(4,),
            in_specs=[pl.BlockSpec((tall, depth), lambda n, at: (n, 0))] * 4
            + [pl.BlockSpec((4, 1, depth), lambda n, at: (0, 0, 0))]
            + [pl.BlockSpec(memory_space=pl.ANY)] * len(before),
            out_specs=pl.BlockSpec((tall, 4 * depth), lambda n, at: ((at[2] ^ j) * 4 + n, 0)),
        ),
        out_shape=jax.ShapeDtypeStruct((4 * tokens, 4 * depth), BF16),
        input_output_aliases={6: 0} if before else {},
        cost_estimate=pl.CostEstimate(
            flops=4 * tokens * depth * 4, bytes_accessed=16 * tokens * depth, transcendentals=tokens
        ),
    )(where_at, *pieces, gain.reshape(4, 1, depth), *before)


def mask_down(weight, wide):
    blocks, _, cols = wide.shape
    tall = weight.shape[0] // blocks

    def kernel(w_ref, mask_ref, out_ref):
        out_ref[...] = w_ref[...] * mask_ref[0]

    return pl.pallas_call(
        kernel,
        grid=(blocks,),
        in_specs=[
            pl.BlockSpec((tall, cols), lambda n: (n, 0)),
            pl.BlockSpec((1, 1, cols), lambda n: (n, 0, 0)),
        ],
        out_specs=pl.BlockSpec((tall, cols), lambda n: (n, 0)),
        out_shape=jax.ShapeDtypeStruct(weight.shape, BF16),
        cost_estimate=pl.CostEstimate(
            flops=weight.size, bytes_accessed=4 * weight.size, transcendentals=0
        ),
    )(weight, wide)


def gate_up(x, dense, where_at, s, n_col):
    tokens, depth = x.shape[0] // n_col, x.shape[1]
    double = dense.shape[1]
    tiles = double // 256

    def kernel(at_ref, x_ref, w_ref, out_ref):
        total = jnp.dot(x_ref[...], w_ref[...], preferred_element_type=F32)
        mine, other = total[:, :128], total[:, 128:]
        gate = jnp.where(at_ref[0] == 0, mine, other)
        up = jnp.where(at_ref[0] == 0, other, mine)
        out_ref[...] = (gate / (1.0 + jnp.exp(-gate)) * up).astype(BF16)

    return pl.pallas_call(
        kernel,
        grid_spec=pltpu.PrefetchScalarGridSpec(
            num_scalar_prefetch=1,
            grid=(tiles,),
            in_specs=[
                pl.BlockSpec((tokens, depth), lambda n, at: (lax.rem(at[2] - s + n_col, n_col), 0)),
                pl.BlockSpec((depth, 256), lambda n, at: (0, n)),
            ],
            out_specs=pl.BlockSpec((tokens, 128), lambda n, at: (0, n)),
        ),
        out_shape=jax.ShapeDtypeStruct((tokens, tiles * 128), BF16),
        cost_estimate=pl.CostEstimate(
            flops=2 * tokens * depth * double,
            bytes_accessed=2 * (tokens * depth + dense.size),
            transcendentals=tokens * tiles * 128,
        ),
    )(where_at, x, dense)


def down_part(pieces, weights, where_at, kind):
    tokens, depth = pieces[0].shape
    n_row, _, cols = weights.shape
    lanes = 256

    def kernel(at_ref, h0, h1, h2, h3, w_ref, out_ref):
        row = at_ref[1]
        total = None
        for m, h in enumerate((h0, h1, h2, h3)):
            part = jnp.dot(h[...], w_ref[row ^ m], preferred_element_type=F32)
            total = part if total is None else total + part
        out_ref[...] = total.astype(kind)

    out_spec = pl.BlockSpec((tokens, lanes), lambda n, at: (0, n))
    return pl.pallas_call(
        kernel,
        grid_spec=pltpu.PrefetchScalarGridSpec(
            num_scalar_prefetch=1,
            grid=(cols // lanes,),
            in_specs=[pl.BlockSpec((tokens, depth), lambda n, at: (0, 0))] * 4
            + [pl.BlockSpec((n_row, depth, lanes), lambda n, at: (0, 0, n))],
            out_specs=out_spec,
        ),
        out_shape=jax.ShapeDtypeStruct((tokens, cols), kind),
        cost_estimate=pl.CostEstimate(
            flops=2 * tokens * n_row * depth * cols,
            bytes_accessed=2 * (4 * tokens * depth + weights.size + tokens * cols * 2),
            transcendentals=0,
        ),
    )(where_at, *pieces, weights)


def body(*args):
    return layer(*args)


def layer(tokens, norm_gain, gate_weight, up_weight, down_weight, block_mask):
    n_row = lax.axis_size("row")
    n_col = lax.axis_size("col")
    group = lax.axis_index("group")
    row = lax.axis_index("row")
    col = lax.axis_index("col")
    n_blocks = block_mask.shape[-1]
    per_col = n_blocks // n_col
    per_row = n_blocks // n_row
    cap = cap_of(per_col)
    rows, cols = gate_weight.shape
    width = cols // n_col

    def beside(by):
        return [(i, i ^ by) for i in range(n_col)]

    swap = [(0, 1), (1, 0)]
    core = [(i, i ^ 1) for i in range(n_row)]
    across = [(i, i ^ 2) for i in range(n_row)]
    grid = [(r, c) for r in range(n_row) for c in range(n_col)]

    def in_plane(m):
        return [(r * n_col + c, (r ^ c ^ m) * n_col + c) for r, c in grid if c != m]

    def to_plane(m):
        return [(r * n_col + c, r * n_col + (r ^ c ^ m)) for r, c in grid if r != m]

    three = lax.iota(jnp.int32, 3)
    where_at = jnp.where(three == 0, group, jnp.where(three == 1, row, col)).astype(jnp.int32)
    grouped = block_mask[:2].reshape(2, n_col, per_col, n_blocks)
    ids = jnp.arange(per_col, dtype=jnp.int32)
    before = (ids[None, :] < ids[:, None]).astype(jnp.int32)
    rank = jnp.sum(before[None, None, :, :, None] * grouped[:, :, None, :, :], axis=3)
    slots = jnp.where(grouped > 0, rank, -1).astype(jnp.int32)
    wanted = jnp.arange(cap, dtype=jnp.int32)
    table = jnp.sum(
        jnp.where(
            slots[:, :, None, :, :] == wanted[None, None, :, None, None],
            ids[None, None, None, :, None],
            0,
        ),
        axis=3,
    ).astype(jnp.int32)
    slots = slots.reshape(-1)
    table = table.reshape(-1)

    far = lax.ppermute(tokens, "col", beside(2))
    near = lax.ppermute(tokens, "col", beside(1))
    shards = [tokens, near, far, lax.ppermute(far, "col", beside(1))]

    def over_row(v):
        far = lax.ppermute(v, "row", across)
        return v, lax.ppermute(v, "row", core), far, lax.ppermute(far, "row", core)

    normed = None
    for i, v in enumerate(shards):
        normed = norm_of(over_row(v), norm_gain, where_at, i, normed)

    sizes = (rows, width, per_col, per_row, n_col, n_blocks)
    order = [0, 2, 1, 3]
    got = {}
    for m in order:
        halves = pack(gate_weight, up_weight, table, where_at, m, per_col, per_row, n_col, n_blocks)
        got[m] = []
        for v in halves:
            v = jnp.where(col == m, v, lax.ppermute(v, ("row", "col"), in_plane(m)))
            came = lax.ppermute(v, ("row", "col"), to_plane(m))
            v = jnp.where(row == m, v, came)
            got[m].append((v, lax.ppermute(v, "group", swap)))
    dense = None
    for m in order:
        (a, b), (c, d) = got[m]
        dense = expand((a, c), (b, d), slots, where_at, m, dense, sizes)
    dense = dense.reshape(-1, dense.shape[-1])

    tile = lax.dynamic_slice(block_mask[2], (col * per_col, row * per_row), (per_col, per_row))
    wide = jnp.repeat(tile.astype(BF16), down_weight.shape[1] // per_row, axis=1)
    weights = mask_down(down_weight, wide[:, None, :])
    weights = weights.reshape(n_row, -1, down_weight.shape[1])

    def part_of(s, kind):
        hidden = gate_up(normed, dense, where_at, s, n_col)
        return down_part(over_row(hidden), weights, where_at, kind)

    ring = [(i, (i + 1) % n_col) for i in range(n_col)]
    passing = lax.ppermute(part_of(1, BF16), "col", ring)
    for s in range(2, n_col):
        passing = (part_of(s, F32) + passing.astype(F32)).astype(BF16)
        passing = lax.ppermute(passing, "col", ring)
    return (part_of(0, F32) + passing.astype(F32)).astype(BF16)


def solution(mesh):
    in_specs = (
        P(("group", "col"), "row"),
        P(),
        P("col", "row"),
        P("col", "row"),
        P("col", "row"),
        P(),
    )
    out_specs = P(("group", "col"), "row")
    sizes = dict(mesh.shape)
    fits = sizes["row"] == 4 and sizes["col"] == 4 and sizes["group"] == 2

    def step(tokens, norm_gain, gate_weight, up_weight, down_weight, block_mask):
        lanes = gate_weight.shape[1] // (sizes["row"] * sizes["col"])
        chosen = body if fits and lanes % 128 == 0 else plain_body
        return jax.shard_map(
            chosen, mesh=mesh, in_specs=in_specs, out_specs=out_specs, check_vma=False
        )(tokens, norm_gain, gate_weight, up_weight, down_weight, block_mask)

    return step
```
